32 devices in a mesh: cluster: 4 (over z), vector: 2 (over y), replica: 4 (over x, core).
Axes of the slice: x: 2, y: 2, z: 4, core: 2. Of those that a mesh axis runs over, the one named last changes fastest.
Arguments:
- samples: bfloat16 [128, 131072], P('vector', ('cluster', 'replica')), may hold values from -6 to 6
- leaf_basis_matrix: bfloat16 [32, 64, 2048], P(None, None, ('cluster', 'replica')), may hold values from -0.75 to 0.75
- transfer: bfloat16 [32, 32, 2048], P(None, None, ('cluster', 'replica')), may hold values from -0.75 to 0.75
- leaf_lists: int32 [4, 2048], P(None, ('cluster', 'replica')), may hold values from 0 to 2047, as said below
- leaf_coupling: bfloat16 [32, 32, 4, 2048], P(None, None, None, ('cluster', 'replica')), may hold values from -0.5 to 0.5
- parent_lists: int32 [4, 1024], P(None, ('cluster', 'replica')), may hold values from 0 to 1023, as said below
- parent_coupling: bfloat16 [32, 32, 4, 1024], P(None, None, None, ('cluster', 'replica')), may hold values from -0.5 to 0.5
- test_matrix: bfloat16 [128, 32], P('vector'), may hold values from -0.5 to 0.5
Outputs:
- product: bfloat16 [128, 131072], P('vector', ('cluster', 'replica'))
- new_basis: float32 [64, 32, 2048], P(None, None, ('cluster', 'replica'))
- fresh_transfer_sketch: float32 [32, 32, 2048], P(None, None, ('cluster', 'replica'))
The draws below stay inside these ranges and needn't reach their ends.
Inputs may be any that keep to these rules, and one draw needn't show every extreme that they name: `leaf_lists`: every source leaf lies within 128 leaves of its target leaf, and some source lies exactly 128 leaves away. `parent_lists`: every source parent lies within half of 128 parents of its target parent, and some source lies exactly that far away.
All inputs are finite; a program needn't handle non-finite values.
Results may differ from the reference program's by a relative error of at most 0.0062.
Values may be sent and summed in bfloat16 or wider, within the bound.
A program may use at most 64 MiB of HBM per device.

```python
import jax
import jax.numpy as jnp
from jax import lax

P_SIZE = 64
R = 32
VEC = 128
LEAF_COUPLINGS = 4
K_PAR = 4
LEAF_DEV = 128
NLEAF = 2048
NPAR = 1024
NPTS = 131072


def near_lists(key, blocks, count, reach):
    targets = jnp.arange(count, dtype=jnp.int32)[None, :]
    offsets = jax.random.randint(key, (blocks, count), -reach, reach + 1, dtype=jnp.int32)
    sources = jnp.clip(targets + offsets, 0, count - 1)
    return sources.at[0, 0].set(reach)


def draw_leaf_lists(key, part):
    return near_lists(jax.random.fold_in(key, 11), LEAF_COUPLINGS, NLEAF, LEAF_DEV)


def draw_parent_lists(key, part):
    return near_lists(jax.random.fold_in(key, 23), K_PAR, NPAR, LEAF_DEV // 2)


def block_scale(stream_key, dims, pieces, least, largest):
    def one(position, blocks):
        draws = jax.random.uniform(jax.random.fold_in(jax.random.fold_in(stream_key, 6), position), (blocks,), jnp.float32, least / len(pieces), largest / len(pieces))
        return jnp.repeat(jnp.exp(draws), dims[position] // blocks).reshape((-1,) + (1,) * (len(dims) - position - 1))

    loudness = one(*pieces[0])
    for cut in pieces[1:]:
        loudness = loudness * one(*cut)
    return loudness


def scatter_about(rng, dims, scale, most, cuts=(), kind=jnp.bfloat16):
    drawn = scale * jax.random.normal(rng, dims, jnp.float32)
    if cuts:
        drawn = drawn * block_scale(rng, dims, cuts, -0.22, 0.18)
    return jnp.clip(drawn, -most, most).astype(kind)


def setup_inputs(seed: int = 0) -> dict:
    streams_of = jax.random.split(jax.random.key(seed), 9)
    return {
        "samples": scatter_about(streams_of[0], (VEC, NPTS), 1.0, 6.0, ((0, 2), (1, 16))),
        "leaf_basis_matrix": scatter_about(streams_of[1], (R, P_SIZE, NLEAF), P_SIZE ** -0.5, 0.75, ((2, 16),)),
        "transfer": scatter_about(streams_of[2], (R, R, NLEAF), (2 * R) ** -0.5, 0.75, ((2, 16),)),
        "leaf_lists": draw_leaf_lists(jax.random.fold_in(streams_of[8], 71), 0),
        "leaf_coupling": scatter_about(streams_of[4], (R, R, LEAF_COUPLINGS, NLEAF), (LEAF_COUPLINGS * R) ** -0.5, 0.5, ((3, 16),)),
        "parent_lists": draw_parent_lists(jax.random.fold_in(streams_of[8], 71), 0),
        "parent_coupling": scatter_about(streams_of[6], (R, R, K_PAR, NPAR), (K_PAR * R) ** -0.5, 0.5, ((3, 16),)),
        "test_matrix": scatter_about(streams_of[7], (VEC, R), VEC ** -0.5, 0.5, ((0, 2),)),
    }


def finish_basis(sketch, width):
    scale = lax.rsqrt(lax.optimization_barrier(jnp.mean(sketch * sketch, axis=0, keepdims=True)) + 1e-06)
    new_basis = sketch * scale
    fresh_transfer_sketch = jnp.einsum('pal,pbl->abl', new_basis, sketch, precision=lax.Precision.HIGHEST) / width
    return (new_basis, fresh_transfer_sketch)

def reference(samples, leaf_basis_matrix, transfer, leaf_lists, leaf_coupling, parent_lists, parent_coupling, test_matrix):
    rank, width, leaves = leaf_basis_matrix.shape
    vectors = samples.shape[0]
    each_leaf_amount = samples.reshape(vectors, leaves, width).astype(jnp.float32)
    leaf_coeff = jnp.einsum('rpl,vlp->rvl', leaf_basis_matrix.astype(jnp.float32), each_leaf_amount).astype(jnp.bfloat16)
    pairs = transfer.astype(jnp.float32).reshape(rank, rank, leaves // 2, 2)
    children = leaf_coeff.astype(jnp.float32).reshape(rank, vectors, leaves // 2, 2)
    parent_coeff = jnp.einsum('abqc,avqc->bvq', pairs, children).astype(jnp.bfloat16)
    leaf_src = leaf_coeff[:, :, leaf_lists].astype(jnp.float32)
    leaf_far = jnp.einsum('rskt,svkt->rvt', leaf_coupling.astype(jnp.float32), leaf_src)
    parent_src = parent_coeff[:, :, parent_lists].astype(jnp.float32)
    parent_far = jnp.einsum('rskq,svkq->rvq', parent_coupling.astype(jnp.float32), parent_src)
    descend = jnp.einsum('abqc,bvq->avqc', pairs, parent_far, precision=lax.Precision.HIGHEST)
    leaf_count_total = (leaf_far + descend.reshape(rank, vectors, leaves)).astype(jnp.bfloat16)
    product = jnp.einsum('etw,ebw->bwt', leaf_basis_matrix.astype(jnp.float32), leaf_count_total.astype(jnp.float32)).astype(jnp.bfloat16)
    sketch = jnp.einsum('vlp,vr->prl', product.astype(jnp.float32), test_matrix.astype(jnp.float32))
    new_basis, fresh_transfer_sketch = finish_basis(sketch, width)
    return (product.reshape(vectors, leaves * width), new_basis, fresh_transfer_sketch)
```

```python
import functools

import jax
import jax.numpy as jnp
from jax import lax
from jax.experimental import pallas as pl
from jax.experimental.pallas import tpu as pltpu
from jax.sharding import PartitionSpec as P

F32 = jnp.float32
BF16 = jnp.bfloat16
LINE = ("cluster", "replica")
TN = (((0,), (0,)), ((), ()))
NT = (((1,), (1,)), ((), ()))


def dot(a, b, dims=(((1,), (0,)), ((), ()))):
    return lax.dot_general(a, b, dims, preferred_element_type=F32)


def block_diagonal(pair):
    first, second = pair[0], pair[1]
    zero = jnp.zeros_like(first)
    return jnp.concatenate(
        [jnp.concatenate([first, zero], axis=1), jnp.concatenate([zero, second], axis=1)], axis=0
    )


def coeff_kernel(samples_ref, basis_ref, down_ref, coeff_ref):
    count, rank = down_ref.shape[0], down_ref.shape[1]
    width = 2 * basis_ref.shape[2]
    half = rank // 2
    for q in range(count):
        both = block_diagonal((basis_ref[2 * q], basis_ref[2 * q + 1]))
        points = samples_ref[:, q * width : (q + 1) * width]
        leaf = dot(both, points, NT).astype(BF16)
        parent = dot(down_ref[q], leaf).astype(BF16)
        coeff_ref[q, :rank, :] = jnp.concatenate([leaf[:rank], leaf[rank:]], axis=1)
        coeff_ref[q, rank:, :] = jnp.concatenate([parent[:half], parent[half:]], axis=1)


def swap_halves(block):
    half = block.shape[1] // 2
    return jnp.concatenate([block[:, half:], block[:, :half]], axis=1)


def far_kernel(
    leaf_lists_ref,
    parent_lists_ref,
    low_ref,
    own_ref,
    high_ref,
    leaf_coupling_ref,
    parent_coupling_ref,
    down_ref,
    basis_ref,
    test_ref,
    product_ref,
    packed_ref,
    leaf_ext,
    parent_ext,
    totals,
):
    step = pl.program_id(0)
    count, rank = down_ref.shape[0], down_ref.shape[1]
    vectors = product_ref.shape[0]
    width = 2 * basis_ref.shape[2]
    parents = own_ref.shape[0]

    @pl.when(step == 0)
    def _():
        for place, ref in enumerate((low_ref, own_ref, high_ref)):

            @pl.loop(0, parents // 4)
            def _(group):
                for u in range(4):
                    q = group * 4 + u
                    target = place * parents + q
                    pair = ref[q, :rank, :]
                    up = ref[q, rank:, :]
                    leaf_ext[2 * target] = pair
                    leaf_ext[2 * target + 1] = swap_halves(pair)
                    parent_ext[target, : rank // 2, :] = up
                    parent_ext[target, rank // 2 :, :] = swap_halves(up)

    for i in range(count):
        q = step * count + i
        far = []
        for c in range(2):
            t = 2 * q + c
            source = jnp.concatenate(
                [leaf_ext[leaf_lists_ref[k, t]] for k in range(leaf_lists_ref.shape[0])], axis=0
            )
            far.append(dot(leaf_coupling_ref[2 * i + c], source))
        source = jnp.concatenate(
            [parent_ext[parent_lists_ref[k, q]] for k in range(parent_lists_ref.shape[0])], axis=0
        )
        parent_far = dot(parent_coupling_ref[i], source).astype(BF16)
        descend = dot(down_ref[i], parent_far, TN)
        total = (jnp.concatenate(far, axis=0) + descend).astype(BF16)
        rows = pl.ds(pl.multiple_of(q * 2 * rank, 2 * rank), 2 * rank)
        totals[rows, :] = total.astype(F32)
        both = block_diagonal((basis_ref[2 * i], basis_ref[2 * i + 1]))
        product_ref[:, i * width : (i + 1) * width] = dot(total[:, :vectors], both, TN).astype(BF16)

    @pl.when(step == pl.num_programs(0) - 1)
    def _():
        for a in range(rank):
            mine = totals[pl.ds(a, 2 * parents, stride=rank), :][:, :vectors].astype(BF16)
            packed_ref[a * rank : (a + 1) * rank, :] = dot(test_ref[...], mine, (((0,), (1,)), ((), ()))).astype(BF16)


def finish_kernel(parts, *refs):
    basis_ref, new_basis_ref, fresh_ref, summed, wide, sketch = refs[parts:]
    rank, width = basis_ref.shape[0], basis_ref.shape[1]
    lanes = basis_ref.shape[2]
    total = refs[0][...].astype(F32)
    for ref in refs[1:parts]:
        total = total + ref[...].astype(F32)
    summed[...] = total
    for a in range(rank):
        wide[a * width : (a + 1) * width, :] = basis_ref[a].astype(F32)
    group = 8

    def points(block, square):
        first = block * group
        acc = [jnp.zeros((rank, lanes), F32) for _ in range(group)]
        for a in range(rank):
            mixed = summed[a * rank : (a + 1) * rank, :]
            for j in range(group):
                acc[j] = acc[j] + wide[pl.ds(a * width + first + j, 1), :] * mixed
        for j in range(group):
            sketch[first + j] = acc[j]
            square = square + acc[j] * acc[j]
        return square

    square = lax.fori_loop(0, width // group, points, jnp.zeros((rank, lanes), F32))
    scale = lax.rsqrt(square / width + 1e-06)
    for p in range(width):
        new_basis_ref[p] = sketch[p] * scale

    def grams(block, carry):
        first = block * group

        acc = [jnp.zeros((rank, lanes), F32) for _ in range(group)]
        for p in range(width):
            row = sketch[p]
            for j in range(group):
                acc[j] = acc[j] + new_basis_ref[p, pl.ds(first + j, 1), :] * row
        for j in range(group):
            fresh_ref[first + j] = acc[j] / width
        return carry

    lax.fori_loop(0, rank // group, grams, 0)


def shards(
    samples,
    leaf_basis_matrix,
    transfer,
    leaf_lists,
    leaf_coupling,
    parent_lists,
    parent_coupling,
    test_matrix,
):
    rank, width, leaves = leaf_basis_matrix.shape
    vectors = samples.shape[0]
    parents = leaves // 2
    leaf_blocks, parent_blocks = leaf_lists.shape[0], parent_lists.shape[0]
    count = 8
    steps = parents // count

    basis = leaf_basis_matrix.transpose(2, 0, 1)
    down = transfer.reshape(rank, rank, parents, 2).transpose(2, 1, 3, 0).reshape(parents, rank, 2 * rank)
    coeff = pl.pallas_call(
        coeff_kernel,
        grid=(steps,),
        in_specs=[
            pl.BlockSpec((vectors, 2 * count * width), lambda i: (0, i)),
            pl.BlockSpec((2 * count, rank, width), lambda i: (i, 0, 0)),
            pl.BlockSpec((count, rank, 2 * rank), lambda i: (i, 0, 0)),
        ],
        out_specs=pl.BlockSpec((count, rank + rank // 2, 2 * vectors), lambda i: (i, 0, 0)),
        out_shape=jax.ShapeDtypeStruct((parents, rank + rank // 2, 2 * vectors), BF16),
        name="coefficients",
    )(samples, basis, down)

    size = lax.axis_size(LINE)
    forward = [(i, i + 1) for i in range(size - 1)]
    backward = [(i + 1, i) for i in range(size - 1)]
    low = lax.ppermute(coeff, LINE, forward)
    high = lax.ppermute(coeff, LINE, backward)

    position = lax.axis_index(LINE)
    leaf_local = leaf_lists - (position - 1) * leaves
    parent_local = parent_lists - (position - 1) * parents
    leaf_mats = leaf_coupling.transpose(3, 0, 2, 1).reshape(leaves, rank, leaf_blocks * rank)
    parent_mats = parent_coupling.transpose(3, 0, 2, 1).reshape(parents, rank, parent_blocks * rank)

    whole = pl.BlockSpec(coeff.shape, lambda i, *_: (0, 0, 0))
    product, packed = pl.pallas_call(
        far_kernel,
        grid_spec=pltpu.PrefetchScalarGridSpec(
            num_scalar_prefetch=2,
            grid=(steps,),
            in_specs=[
                whole,
                whole,
                whole,
                pl.BlockSpec((2 * count, rank, leaf_blocks * rank), lambda i, *_: (i, 0, 0)),
                pl.BlockSpec((count, rank, parent_blocks * rank), lambda i, *_: (i, 0, 0)),
                pl.BlockSpec((count, rank, 2 * rank), lambda i, *_: (i, 0, 0)),
                pl.BlockSpec((2 * count, rank, width), lambda i, *_: (i, 0, 0)),
                pl.BlockSpec(test_matrix.shape, lambda i, *_: (0, 0)),
            ],
            out_specs=[
                pl.BlockSpec((vectors, 2 * count * width), lambda i, *_: (0, i)),
                pl.BlockSpec((rank * rank, leaves), lambda i, *_: (0, 0)),
            ],
            scratch_shapes=[
                pltpu.VMEM((3 * leaves, rank, 2 * vectors), BF16),
                pltpu.VMEM((3 * parents, rank, 2 * vectors), BF16),
                pltpu.VMEM((leaves * rank, 2 * vectors), F32),
            ],
        ),
        out_shape=[
            jax.ShapeDtypeStruct(samples.shape, BF16),
            jax.ShapeDtypeStruct((rank * rank, leaves), BF16),
        ],
        name="far_field",
    )(leaf_local, parent_local, low, coeff, high, leaf_mats, parent_mats, down, basis, test_matrix)

    if lax.axis_size("vector") == 2:
        pieces = (packed, lax.ppermute(packed, "vector", [(0, 1), (1, 0)]))
    else:
        pieces = (lax.psum(packed.astype(F32), "vector"),)
    new_basis, fresh = pl.pallas_call(
        functools.partial(finish_kernel, len(pieces)),
        in_specs=[pl.BlockSpec(memory_space=pltpu.VMEM)] * (len(pieces) + 1),
        out_specs=[pl.BlockSpec(memory_space=pltpu.VMEM)] * 2,
        out_shape=[
            jax.ShapeDtypeStruct((width, rank, leaves), F32),
            jax.ShapeDtypeStruct((rank, rank, leaves), F32),
        ],
        scratch_shapes=[
            pltpu.VMEM((rank * rank, leaves), F32),
            pltpu.VMEM((rank * width, leaves), F32),
            pltpu.VMEM((width, rank, leaves), F32),
        ],
        name="finish",
    )(*pieces, leaf_basis_matrix)
    return product, new_basis, fresh


def solution(mesh):
    placed = (
        P("vector", LINE),
        P(None, None, LINE),
        P(None, None, LINE),
        P(None, LINE),
        P(None, None, None, LINE),
        P(None, LINE),
        P(None, None, None, LINE),
        P("vector", None),
    )
    return jax.shard_map(
        shards,
        mesh=mesh,
        in_specs=placed,
        out_specs=(P("vector", LINE), P(None, None, LINE), P(None, None, LINE)),
        check_vma=False,
    )
```

```python
import functools

import jax
import jax.numpy as jnp
from jax import lax
from jax.experimental import pallas as pl
from jax.experimental.pallas import tpu as pltpu
from jax.sharding import PartitionSpec as P

F32 = jnp.float32
BF16 = jnp.bfloat16
LINE = ("cluster", "replica")
TN = (((0,), (0,)), ((), ()))
NT = (((1,), (1,)), ((), ()))


def dot(a, b, dims=(((1,), (0,)), ((), ()))):
    return lax.dot_general(a, b, dims, preferred_element_type=F32)


def block_diagonal(pair):
    first, second = pair[0], pair[1]
    zero = jnp.zeros_like(first)
    return jnp.concatenate(
        [jnp.concatenate([first, zero], axis=1), jnp.concatenate([zero, second], axis=1)], axis=0
    )


def coeff_kernel(samples_ref, basis_ref, up_ref, coeff_ref):
    count, rank = up_ref.shape[0], basis_ref.shape[1]
    width = 2 * basis_ref.shape[2]
    half = rank // 2
    leaves = []
    for q in range(count):
        both = block_diagonal((basis_ref[2 * q], basis_ref[2 * q + 1]))
        points = samples_ref[:, q * width : (q + 1) * width]
        leaves.append(dot(both, points, NT).astype(BF16))
    parents = [dot(up_ref[q], leaves[q], TN).astype(BF16) for q in range(count)]
    for q in range(count):
        leaf, parent = leaves[q], parents[q]
        coeff_ref[q, :rank, :] = jnp.concatenate([leaf[:rank], leaf[rank:]], axis=1)
        coeff_ref[q, rank:, :] = jnp.concatenate([parent[:half], parent[half:]], axis=1)


def swap_halves(block):
    half = block.shape[1] // 2
    return jnp.concatenate([block[:, half:], block[:, :half]], axis=1)


def far_kernel(
    leaf_lists_ref,
    parent_lists_ref,
    low_ref,
    own_ref,
    high_ref,
    leaf_coupling_ref,
    parent_coupling_ref,
    up_ref,
    basis_ref,
    test_ref,
    product_ref,
    packed_ref,
    leaf_ext,
    parent_ext,
    totals,
):
    step = pl.program_id(0)
    count, rank = up_ref.shape[0], basis_ref.shape[1]
    vectors = product_ref.shape[0]
    width = 2 * basis_ref.shape[2]
    parents = own_ref.shape[0]

    @pl.when(step == 0)
    def _():
        for place, ref in enumerate((low_ref, own_ref, high_ref)):

            @pl.loop(0, parents // 4)
            def _(group):
                for u in range(4):
                    q = group * 4 + u
                    target = place * parents + q
                    pair = ref[q, :rank, :]
                    up = ref[q, rank:, :]
                    leaf_ext[2 * target] = pair
                    leaf_ext[2 * target + 1] = swap_halves(pair)
                    parent_ext[target, : rank // 2, :] = up
                    parent_ext[target, rank // 2 :, :] = swap_halves(up)

    before = lax.axis_index(LINE) - 1
    leaf_first, parent_first = before * (2 * parents), before * parents
    leaf_far, parent_far = [], []
    for i in range(count):
        q = step * count + i
        for c in range(2):
            source = jnp.concatenate(
                [leaf_ext[leaf_lists_ref[k, 2 * q + c] - leaf_first] for k in range(leaf_lists_ref.shape[0])],
                axis=0,
            )
            leaf_far.append(dot(leaf_coupling_ref[2 * i + c], source))
        source = jnp.concatenate(
            [parent_ext[parent_lists_ref[k, q] - parent_first] for k in range(parent_lists_ref.shape[0])], axis=0
        )
        parent_far.append(dot(parent_coupling_ref[i], source).astype(BF16))
    descend = [dot(up_ref[i], parent_far[i]) for i in range(count)]
    total = []
    for i in range(count):
        far = jnp.concatenate(leaf_far[2 * i : 2 * i + 2], axis=0)
        total.append((far + descend[i]).astype(BF16))
    for i in range(count):
        both = block_diagonal((basis_ref[2 * i], basis_ref[2 * i + 1]))
        product_ref[:, i * width : (i + 1) * width] = dot(total[i][:, :vectors], both, TN).astype(BF16)
    for i in range(count):
        rows = pl.ds(pl.multiple_of((step * count + i) * 2 * rank, 2 * rank), 2 * rank)
        totals[rows, :] = total[i].astype(F32)

    @pl.when(step == pl.num_programs(0) - 1)
    def _():
        for a in range(rank):
            mine = totals[pl.ds(a, 2 * parents, stride=rank), :][:, :vectors].astype(BF16)
            packed_ref[a * rank : (a + 1) * rank, :] = dot(test_ref[...], mine, NT).astype(BF16)


def finish_kernel(parts, *refs):
    basis_ref, new_basis_ref, fresh_ref, summed, wide, sketch = refs[parts:]
    rank, width = basis_ref.shape[0], basis_ref.shape[1]
    lanes = basis_ref.shape[2]
    total = refs[0][...].astype(F32)
    for ref in refs[1:parts]:
        total = total + ref[...].astype(F32)
    summed[...] = total
    for a in range(rank):
        wide[a * width : (a + 1) * width, :] = basis_ref[a].astype(F32)
    group = 8

    def points(block, square):
        first = block * group
        acc = [jnp.zeros((rank, lanes), F32) for _ in range(group)]
        for a in range(rank):
            mixed = summed[a * rank : (a + 1) * rank, :]
            for j in range(group):
                acc[j] = acc[j] + wide[pl.ds(a * width + first + j, 1), :] * mixed
        for j in range(group):
            sketch[first + j] = acc[j]
            square = square + acc[j] * acc[j]
        return square

    square = lax.fori_loop(0, width // group, points, jnp.zeros((rank, lanes), F32))
    scale = lax.rsqrt(square / width + 1e-06)
    for p in range(width):
        new_basis_ref[p] = sketch[p] * scale

    def grams(block, carry):
        first = block * group

        acc = [jnp.zeros((rank, lanes), F32) for _ in range(group)]
        for p in range(width):
            row = sketch[p]
            for j in range(group):
                acc[j] = acc[j] + new_basis_ref[p, pl.ds(first + j, 1), :] * row
        for j in range(group):
            fresh_ref[first + j] = acc[j] / width
        return carry

    lax.fori_loop(0, rank // group, grams, 0)


def shards(
    samples,
    leaf_basis_matrix,
    transfer,
    leaf_lists,
    leaf_coupling,
    parent_lists,
    parent_coupling,
    test_matrix,
):
    rank, width, leaves = leaf_basis_matrix.shape
    vectors = samples.shape[0]
    parents = leaves // 2
    leaf_blocks, parent_blocks = leaf_lists.shape[0], parent_lists.shape[0]
    count = 16 if parents % 16 == 0 else parents
    steps = parents // count

    basis = leaf_basis_matrix.transpose(2, 0, 1)
    up = transfer.transpose(2, 0, 1).reshape(parents, 2 * rank, rank)
    test = test_matrix.T
    coeff = pl.pallas_call(
        coeff_kernel,
        grid=(steps,),
        in_specs=[
            pl.BlockSpec((vectors, 2 * count * width), lambda i: (0, i)),
            pl.BlockSpec((2 * count, rank, width), lambda i: (i, 0, 0)),
            pl.BlockSpec((count, 2 * rank, rank), lambda i: (i, 0, 0)),
        ],
        out_specs=pl.BlockSpec((count, rank + rank // 2, 2 * vectors), lambda i: (i, 0, 0)),
        out_shape=jax.ShapeDtypeStruct((parents, rank + rank // 2, 2 * vectors), BF16),
        name="coefficients",
    )(samples, basis, up)

    size = lax.axis_size(LINE)
    forward = [(i, i + 1) for i in range(size - 1)]
    backward = [(i + 1, i) for i in range(size - 1)]
    low = lax.ppermute(coeff, LINE, forward)
    high = lax.ppermute(coeff, LINE, backward)

    leaf_mats = leaf_coupling.transpose(3, 0, 2, 1).reshape(leaves, rank, leaf_blocks * rank)
    parent_mats = parent_coupling.transpose(3, 0, 2, 1).reshape(parents, rank, parent_blocks * rank)

    whole = pl.BlockSpec(coeff.shape, lambda i, *_: (0, 0, 0))
    product, packed = pl.pallas_call(
        far_kernel,
        grid_spec=pltpu.PrefetchScalarGridSpec(
            num_scalar_prefetch=2,
            grid=(steps,),
            in_specs=[
                whole,
                whole,
                whole,
                pl.BlockSpec((2 * count, rank, leaf_blocks * rank), lambda i, *_: (i, 0, 0)),
                pl.BlockSpec((count, rank, parent_blocks * rank), lambda i, *_: (i, 0, 0)),
                pl.BlockSpec((count, 2 * rank, rank), lambda i, *_: (i, 0, 0)),
                pl.BlockSpec((2 * count, rank, width), lambda i, *_: (i, 0, 0)),
                pl.BlockSpec(test.shape, lambda i, *_: (0, 0)),
            ],
            out_specs=[
                pl.BlockSpec((vectors, 2 * count * width), lambda i, *_: (0, i)),
                pl.BlockSpec((rank * rank, leaves), lambda i, *_: (0, 0)),
            ],
            scratch_shapes=[
                pltpu.VMEM((3 * leaves, rank, 2 * vectors), BF16),
                pltpu.VMEM((3 * parents, rank, 2 * vectors), BF16),
                pltpu.VMEM((leaves * rank, 2 * vectors), F32),
            ],
        ),
        out_shape=[
            jax.ShapeDtypeStruct(samples.shape, BF16),
            jax.ShapeDtypeStruct((rank * rank, leaves), BF16),
        ],
        name="far_field",
    )(leaf_lists, parent_lists, low, coeff, high, leaf_mats, parent_mats, up, basis, test)

    if lax.axis_size("vector") == 2:
        pieces = (packed, lax.ppermute(packed, "vector", [(0, 1), (1, 0)]))
    else:
        pieces = (lax.psum(packed.astype(F32), "vector"),)
    new_basis, fresh = pl.pallas_call(
        functools.partial(finish_kernel, len(pieces)),
        in_specs=[pl.BlockSpec(memory_space=pltpu.VMEM)] * (len(pieces) + 1),
        out_specs=[pl.BlockSpec(memory_space=pltpu.VMEM)] * 2,
        out_shape=[
            jax.ShapeDtypeStruct((width, rank, leaves), F32),
            jax.ShapeDtypeStruct((rank, rank, leaves), F32),
        ],
        scratch_shapes=[
            pltpu.VMEM((rank * rank, leaves), F32),
            pltpu.VMEM((rank * width, leaves), F32),
            pltpu.VMEM((width, rank, leaves), F32),
        ],
        name="finish",
    )(*pieces, leaf_basis_matrix)
    return product, new_basis, fresh


def solution(mesh):
    placed = (
        P("vector", LINE),
        P(None, None, LINE),
        P(None, None, LINE),
        P(None, LINE),
        P(None, None, None, LINE),
        P(None, LINE),
        P(None, None, None, LINE),
        P("vector", None),
    )
    return jax.shard_map(
        shards,
        mesh=mesh,
        in_specs=placed,
        out_specs=(P("vector", LINE), P(None, None, LINE), P(None, None, LINE)),
        check_vma=False,
    )
```

```python
import functools

import jax
import jax.numpy as jnp
from jax import lax
from jax.experimental import pallas as pl
from jax.experimental.pallas import tpu as pltpu
from jax.sharding import PartitionSpec as P

F32 = jnp.float32
BF16 = jnp.bfloat16
LINE = ("cluster", "replica")
TN = (((0,), (0,)), ((), ()))
NT = (((1,), (1,)), ((), ()))


def dot(a, b, dims=(((1,), (0,)), ((), ()))):
    return lax.dot_general(a, b, dims, preferred_element_type=F32)


def block_diagonal(pair):
    first, second = pair[0], pair[1]
    zero = jnp.zeros_like(first)
    return jnp.concatenate(
        [jnp.concatenate([first, zero], axis=1), jnp.concatenate([zero, second], axis=1)], axis=0
    )


def swap_halves(block):
    half = block.shape[1] // 2
    return jnp.concatenate([block[:, half:], block[:, :half]], axis=1)


def near(source, first, count):
    return jnp.minimum(jnp.maximum(source - first, 0), count - 1)


def sources_kernel(
    group,
    leaf_lists_ref,
    parent_lists_ref,
    samples_ref,
    basis_ref,
    up_ref,
    leaf_coupling_ref,
    parent_coupling_ref,
    test_ref,
    product_ref,
    packed_ref,
    coeff,
    leaf_ext,
    parent_ext,
    totals,
    leaf_mats,
    parent_mats,
    send_sem,
    recv_sem,
):
    parents, rank = up_ref.shape[0], basis_ref.shape[1]
    leaves = 2 * parents
    vectors = product_ref.shape[0]
    width = 2 * basis_ref.shape[2]
    half = rank // 2
    chunks = parents // group
    leaf_blocks, parent_blocks = leaf_lists_ref.shape[0], parent_lists_ref.shape[0]

    replicas = lax.axis_size("replica")
    size = lax.axis_size("cluster") * replicas
    here = lax.axis_index("cluster") * replicas + lax.axis_index("replica")
    vector = lax.axis_index("vector")

    def device(place):
        return (place // replicas, vector, lax.rem(place, replicas))

    right = device(lax.rem(here + 1, size))
    left = device(lax.rem(here + size - 1, size))

    barrier = pltpu.get_barrier_semaphore()
    for neighbour in (left, right):
        pl.semaphore_signal(barrier, inc=1, device_id=neighbour, device_id_type=pl.DeviceIdType.MESH)
    pl.semaphore_wait(barrier, 2)

    def copies(chunk):
        rows = pl.ds(chunk * group, group)
        return [
            pltpu.make_async_remote_copy(
                src_ref=coeff.at[1, rows],
                dst_ref=coeff.at[slot, rows],
                send_sem=send_sem.at[way, chunk],
                recv_sem=recv_sem.at[way, chunk],
                device_id=target,
                device_id_type=pl.DeviceIdType.MESH,
            )
            for way, (slot, target) in enumerate(((0, right), (2, left)))
        ]

    def coefficients(chunk, carry):
        leaf, parent = [], []
        for j in range(group):
            q = chunk * group + j
            both = block_diagonal((basis_ref[2 * q], basis_ref[2 * q + 1]))
            points = samples_ref[:, pl.ds(pl.multiple_of(q * width, width), width)]
            leaf.append(dot(both, points, NT).astype(BF16))
        for j in range(group):
            parent.append(dot(up_ref[chunk * group + j], leaf[j], TN).astype(BF16))
        for j in range(group):
            q = chunk * group + j
            coeff[1, q, :rank, :] = jnp.concatenate([leaf[j][:rank], leaf[j][rank:]], axis=1)
            coeff[1, q, rank:, :] = jnp.concatenate([parent[j][:half], parent[j][half:]], axis=1)
        for copy in copies(chunk):
            copy.start()
        return carry

    lax.fori_loop(0, chunks, coefficients, 0)

    def relayout(block, carry):
        for u in range(4):
            r = block * 4 + u
            leaf_mats[pl.ds(r, leaves, stride=rank), :] = leaf_coupling_ref[r].astype(F32).T
            parent_mats[pl.ds(r, parents, stride=rank), :] = parent_coupling_ref[r].astype(F32).T
        return carry

    lax.fori_loop(0, rank // 4, relayout, 0)

    def unpack(place, first, many):
        def some(block, carry):
            for u in range(8):
                q = first + block * 8 + u
                target = place * parents + q
                pair = coeff[place, q, :rank, :]
                up = coeff[place, q, rank:, :]
                leaf_ext[2 * target] = pair
                leaf_ext[2 * target + 1] = swap_halves(pair)
                parent_ext[target, :half, :] = up
                parent_ext[target, half:, :] = swap_halves(up)
            return carry

        lax.fori_loop(0, many // 8, some, 0)

    unpack(1, 0, parents)

    def arrive(chunk, carry):
        for copy, place in zip(copies(chunk), (0, 2)):
            copy.wait()
            unpack(place, chunk * group, group)
        return carry

    lax.fori_loop(0, chunks, arrive, 0)

    leaf_first, parent_first = (here - 1) * leaves, (here - 1) * parents

    def far_field(chunk, carry):
        leaf_far, parent_far, total = [], [], []
        for j in range(group):
            q = chunk * group + j
            for c in range(2):
                t = 2 * q + c
                source = jnp.concatenate(
                    [leaf_ext[near(leaf_lists_ref[k, t], leaf_first, 3 * leaves)] for k in range(leaf_blocks)], axis=0
                )
                mats = leaf_mats[pl.ds(pl.multiple_of(t * rank, rank), rank), :].astype(BF16)
                leaf_far.append(dot(mats, source))
            source = jnp.concatenate(
                [parent_ext[near(parent_lists_ref[k, q], parent_first, 3 * parents)] for k in range(parent_blocks)],
                axis=0,
            )
            mats = parent_mats[pl.ds(pl.multiple_of(q * rank, rank), rank), :].astype(BF16)
            parent_far.append(dot(mats, source).astype(BF16))
        descend = [dot(up_ref[chunk * group + j], parent_far[j]) for j in range(group)]
        for j in range(group):
            far = jnp.concatenate(leaf_far[2 * j : 2 * j + 2], axis=0)
            total.append((far + descend[j]).astype(BF16))
        for j in range(group):
            q = chunk * group + j
            both = block_diagonal((basis_ref[2 * q], basis_ref[2 * q + 1]))
            columns = pl.ds(pl.multiple_of(q * width, width), width)
            product_ref[:, columns] = dot(total[j][:, :vectors], both, TN).astype(BF16)
        for j in range(group):
            q = chunk * group + j
            totals[pl.ds(pl.multiple_of(q * 2 * rank, 2 * rank), 2 * rank), :] = total[j].astype(F32)
        return carry

    lax.fori_loop(0, chunks, far_field, 0)

    def pack(block, carry):
        for u in range(8):
            a = block * 8 + u
            mine = totals[pl.ds(a, leaves, stride=rank), :][:, :vectors].astype(BF16)
            rows = pl.ds(pl.multiple_of(a * rank, rank), rank)
            packed_ref[rows, :] = dot(test_ref[...], mine, NT).astype(BF16)
        return carry

    lax.fori_loop(0, rank // 8, pack, 0)


def finish_kernel(parts, *refs):
    basis_ref, new_basis_ref, fresh_ref, summed, wide, sketch = refs[parts:]
    rank, width = basis_ref.shape[0], basis_ref.shape[1]
    lanes = basis_ref.shape[2]
    total = refs[0][...].astype(F32)
    for ref in refs[1:parts]:
        total = total + ref[...].astype(F32)
    summed[...] = total
    for a in range(rank):
        wide[a * width : (a + 1) * width, :] = basis_ref[a].astype(F32)
    group = 8

    def points(block, square):
        first = block * group
        acc = [jnp.zeros((rank, lanes), F32) for _ in range(group)]
        for a in range(rank):
            mixed = summed[a * rank : (a + 1) * rank, :]
            for j in range(group):
                acc[j] = acc[j] + wide[pl.ds(a * width + first + j, 1), :] * mixed
        for j in range(group):
            sketch[first + j] = acc[j]
            square = square + acc[j] * acc[j]
        return square

    square = lax.fori_loop(0, width // group, points, jnp.zeros((rank, lanes), F32))
    scale = lax.rsqrt(square / width + 1e-06)
    for p in range(width):
        new_basis_ref[p] = sketch[p] * scale

    def grams(block, carry):
        first = block * group

        acc = [jnp.zeros((rank, lanes), F32) for _ in range(group)]
        for p in range(width):
            row = sketch[p]
            for j in range(group):
                acc[j] = acc[j] + new_basis_ref[p, pl.ds(first + j, 1), :] * row
        for j in range(group):
            fresh_ref[first + j] = acc[j] / width
        return carry

    lax.fori_loop(0, rank // group, grams, 0)


def shards(
    samples,
    leaf_basis_matrix,
    transfer,
    leaf_lists,
    leaf_coupling,
    parent_lists,
    parent_coupling,
    test_matrix,
):
    rank, width, leaves = leaf_basis_matrix.shape
    vectors = samples.shape[0]
    parents = leaves // 2
    leaf_blocks, parent_blocks = leaf_lists.shape[0], parent_lists.shape[0]
    group = 16 if parents % 16 == 0 else parents
    chunks = parents // group
    leaf_sums, parent_sums = leaf_blocks * rank, parent_blocks * rank

    basis = leaf_basis_matrix.transpose(2, 0, 1)
    up = transfer.transpose(2, 0, 1).reshape(parents, 2 * rank, rank)
    test = test_matrix.T
    leaf_blocks_first = leaf_coupling.transpose(0, 2, 1, 3).reshape(rank, leaf_sums, leaves)
    parent_blocks_first = parent_coupling.transpose(0, 2, 1, 3).reshape(rank, parent_sums, parents)

    product, packed = pl.pallas_call(
        functools.partial(sources_kernel, group),
        in_specs=[pl.BlockSpec(memory_space=pltpu.SMEM)] * 2 + [pl.BlockSpec(memory_space=pltpu.VMEM)] * 6,
        out_specs=[pl.BlockSpec(memory_space=pltpu.VMEM)] * 2,
        out_shape=[
            jax.ShapeDtypeStruct(samples.shape, BF16),
            jax.ShapeDtypeStruct((rank * rank, leaves), BF16),
        ],
        scratch_shapes=[
            pltpu.VMEM((3, parents, rank + rank // 2, 2 * vectors), BF16),
            pltpu.VMEM((3 * leaves, rank, 2 * vectors), BF16),
            pltpu.VMEM((3 * parents, rank, 2 * vectors), BF16),
            pltpu.VMEM((leaves * rank, 2 * vectors), F32),
            pltpu.VMEM((leaves * rank, leaf_sums), F32),
            pltpu.VMEM((parents * rank, parent_sums), F32),
            pltpu.SemaphoreType.DMA((2, chunks)),
            pltpu.SemaphoreType.DMA((2, chunks)),
        ],
        compiler_params=pltpu.CompilerParams(collective_id=0, has_side_effects=True),
        name="far_field",
    )(leaf_lists, parent_lists, samples, basis, up, leaf_blocks_first, parent_blocks_first, test)

    if lax.axis_size("vector") == 2:
        pieces = (packed, lax.ppermute(packed, "vector", [(0, 1), (1, 0)]))
    else:
        pieces = (lax.psum(packed.astype(F32), "vector"),)
    new_basis, fresh = pl.pallas_call(
        functools.partial(finish_kernel, len(pieces)),
        in_specs=[pl.BlockSpec(memory_space=pltpu.VMEM)] * (len(pieces) + 1),
        out_specs=[pl.BlockSpec(memory_space=pltpu.VMEM)] * 2,
        out_shape=[
            jax.ShapeDtypeStruct((width, rank, leaves), F32),
            jax.ShapeDtypeStruct((rank, rank, leaves), F32),
        ],
        scratch_shapes=[
            pltpu.VMEM((rank * rank, leaves), F32),
            pltpu.VMEM((rank * width, leaves), F32),
            pltpu.VMEM((width, rank, leaves), F32),
        ],
        name="finish",
    )(*pieces, leaf_basis_matrix)
    return product, new_basis, fresh


def solution(mesh):
    placed = (
        P("vector", LINE),
        P(None, None, LINE),
        P(None, None, LINE),
        P(None, LINE),
        P(None, None, None, LINE),
        P(None, LINE),
        P(None, None, None, LINE),
        P("vector", None),
    )
    return jax.shard_map(
        shards,
        mesh=mesh,
        in_specs=placed,
        out_specs=(P("vector", LINE), P(None, None, LINE), P(None, None, LINE)),
        check_vma=False,
    )
```

```python
import functools

import jax
import jax.numpy as jnp
from jax import lax
from jax.experimental import pallas as pl
from jax.experimental.pallas import tpu as pltpu
from jax.sharding import PartitionSpec as P

F32 = jnp.float32
BF16 = jnp.bfloat16
LINE = ("cluster", "replica")
TN = (((0,), (0,)), ((), ()))
NT = (((1,), (1,)), ((), ()))


def dot(a, b, dims=(((1,), (0,)), ((), ()))):
    return lax.dot_general(a, b, dims, preferred_element_type=F32)


def block_diagonal(pair):
    first, second = pair[0], pair[1]
    zero = jnp.zeros_like(first)
    return jnp.concatenate(
        [jnp.concatenate([first, zero], axis=1), jnp.concatenate([zero, second], axis=1)], axis=0
    )


def swap_halves(block):
    half = block.shape[1] // 2
    return jnp.concatenate([block[:, half:], block[:, :half]], axis=1)


def blocks_first(block):
    sources, blocks, targets = block.shape
    return jnp.swapaxes(block.astype(F32), 0, 1).reshape(blocks * sources, targets).T


def near(source, first, count):
    return jnp.minimum(jnp.maximum(source - first, 0), count - 1)


def sources_kernel(
    group,
    leaf_lists_ref,
    parent_lists_ref,
    samples_ref,
    basis_ref,
    transfer_ref,
    leaf_coupling_ref,
    parent_coupling_ref,
    test_ref,
    product_ref,
    summed_ref,
    coeff,
    mats,
    leaf_ext,
    parent_ext,
    totals,
    leaf_mats,
    parent_mats,
    own_packed,
    peer_packed,
    send_sem,
    recv_sem,
    packed_send_sem,
    packed_recv_sem,
):
    rank, each, leaves = basis_ref.shape
    parents = leaves // 2
    vectors = product_ref.shape[0]
    width = 2 * each
    paired = lax.axis_size("vector") == 2
    half = rank // 2
    chunks = parents // group
    leaf_blocks, parent_blocks = leaf_lists_ref.shape[0], parent_lists_ref.shape[0]

    replicas = lax.axis_size("replica")
    size = lax.axis_size("cluster") * replicas
    here = lax.axis_index("cluster") * replicas + lax.axis_index("replica")
    vector = lax.axis_index("vector")

    def device(place):
        return (place // replicas, vector, lax.rem(place, replicas))

    right = device(lax.rem(here + 1, size))
    left = device(lax.rem(here + size - 1, size))

    barrier = pltpu.get_barrier_semaphore()
    peer = (lax.axis_index("cluster"), 1 - vector, lax.axis_index("replica"))
    greeted = (left, right, peer) if paired else (left, right)
    for neighbour in greeted:
        pl.semaphore_signal(barrier, inc=1, device_id=neighbour, device_id_type=pl.DeviceIdType.MESH)

    def by_leaf(block, carry):
        for u in range(4):
            r = block * 4 + u
            both = jnp.concatenate([basis_ref[r], transfer_ref[r]], axis=0).astype(F32)
            mats[pl.ds(r, leaves, stride=rank), :] = both.T
        return carry

    lax.fori_loop(0, rank // 4, by_leaf, 0)
    pl.semaphore_wait(barrier, len(greeted))

    def pair_of(q):
        return mats[pl.ds(pl.multiple_of(q * 2 * rank, 2 * rank), 2 * rank), :].astype(BF16)

    def bases(q):
        pair = pair_of(q)[:, :each]
        return block_diagonal((pair[:rank], pair[rank:]))

    def lift(q):
        return pair_of(q)[:, each:]

    def copies(chunk):
        rows = pl.ds(chunk * group, group)
        return [
            pltpu.make_async_remote_copy(
                src_ref=coeff.at[1, rows],
                dst_ref=coeff.at[slot, rows],
                send_sem=send_sem.at[way, chunk],
                recv_sem=recv_sem.at[way, chunk],
                device_id=target,
                device_id_type=pl.DeviceIdType.MESH,
            )
            for way, (slot, target) in enumerate(((0, right), (2, left)))
        ]

    def packed_copy(chunk):
        return pltpu.make_async_remote_copy(
            src_ref=own_packed.at[chunk],
            dst_ref=peer_packed.at[chunk],
            send_sem=packed_send_sem.at[chunk],
            recv_sem=packed_recv_sem.at[chunk],
            device_id=peer,
            device_id_type=pl.DeviceIdType.MESH,
        )

    def coefficients(chunk, carry):
        leaf, parent = [], []
        for j in range(group):
            q = chunk * group + j
            points = samples_ref[:, pl.ds(pl.multiple_of(q * width, width), width)]
            leaf.append(dot(bases(q), points, NT).astype(BF16))
        for j in range(group):
            parent.append(dot(lift(chunk * group + j), leaf[j], TN).astype(BF16))
        for j in range(group):
            q = chunk * group + j
            coeff[1, q, :rank, :] = jnp.concatenate([leaf[j][:rank], leaf[j][rank:]], axis=1)
            coeff[1, q, rank:, :] = jnp.concatenate([parent[j][:half], parent[j][half:]], axis=1)
        for copy in copies(chunk):
            copy.start()
        return carry

    lax.fori_loop(0, chunks, coefficients, 0)

    def relayout(block, carry):
        for u in range(4):
            r = block * 4 + u
            leaf_mats[pl.ds(r, leaves, stride=rank), :] = blocks_first(leaf_coupling_ref[r])
            parent_mats[pl.ds(r, parents, stride=rank), :] = blocks_first(parent_coupling_ref[r])
        return carry

    lax.fori_loop(0, rank // 4, relayout, 0)

    def unpack(place, first, many):
        def some(block, carry):
            for u in range(8):
                q = first + block * 8 + u
                target = place * parents + q
                pair = coeff[place, q, :rank, :]
                up = coeff[place, q, rank:, :]
                leaf_ext[2 * target] = pair
                leaf_ext[2 * target + 1] = swap_halves(pair)
                parent_ext[target, :half, :] = up
                parent_ext[target, half:, :] = swap_halves(up)
            return carry

        lax.fori_loop(0, many // 8, some, 0)

    unpack(1, 0, parents)

    def arrive(chunk, carry):
        for copy, place in zip(copies(chunk), (0, 2)):
            copy.wait()
            unpack(place, chunk * group, group)
        return carry

    lax.fori_loop(0, chunks, arrive, 0)

    leaf_first, parent_first = (here - 1) * leaves, (here - 1) * parents

    def far_field(chunk, carry):
        leaf_far, parent_far, total = [], [], []
        for j in range(group):
            q = chunk * group + j
            for c in range(2):
                t = 2 * q + c
                source = jnp.concatenate(
                    [leaf_ext[near(leaf_lists_ref[k, t], leaf_first, 3 * leaves)] for k in range(leaf_blocks)], axis=0
                )
                mats = leaf_mats[pl.ds(pl.multiple_of(t * rank, rank), rank), :].astype(BF16)
                leaf_far.append(dot(mats, source))
            source = jnp.concatenate(
                [parent_ext[near(parent_lists_ref[k, q], parent_first, 3 * parents)] for k in range(parent_blocks)],
                axis=0,
            )
            mats = parent_mats[pl.ds(pl.multiple_of(q * rank, rank), rank), :].astype(BF16)
            parent_far.append(dot(mats, source).astype(BF16))
        descend = [dot(lift(chunk * group + j), parent_far[j]) for j in range(group)]
        for j in range(group):
            far = jnp.concatenate(leaf_far[2 * j : 2 * j + 2], axis=0)
            total.append((far + descend[j]).astype(BF16))
        for j in range(group):
            q = chunk * group + j
            columns = pl.ds(pl.multiple_of(q * width, width), width)
            product_ref[:, columns] = dot(total[j][:, :vectors], bases(q), TN).astype(BF16)
        for j in range(group):
            q = chunk * group + j
            totals[pl.ds(pl.multiple_of(q * 2 * rank, 2 * rank), 2 * rank), :] = total[j].astype(F32)
        first = chunk * (group * 2 * rank)
        for block in range(rank // chunks):
            mine = jnp.concatenate(
                [totals[pl.ds(first + block * chunks + j, 2 * group, stride=rank), :] for j in range(chunks)], axis=0
            )
            mine = mine[:, :vectors].astype(BF16)
            own_packed[chunk, block * rank : (block + 1) * rank, :] = dot(test_ref[...], mine, NT).astype(BF16)
        if paired:
            packed_copy(chunk).start()
        return carry

    lax.fori_loop(0, chunks, far_field, 0)

    if paired:
        for chunk in range(chunks):
            packed_copy(chunk).wait()
    for block in range(rank // chunks):
        rows = slice(block * rank, (block + 1) * rank)
        parts = [own_packed[chunk, rows, :].astype(F32) for chunk in range(chunks)]
        if paired:
            parts = [parts[chunk] + peer_packed[chunk, rows, :].astype(F32) for chunk in range(chunks)]
        for j in range(chunks):
            lanes = slice(j * 2 * group, (j + 1) * 2 * group)
            a = block * chunks + j
            summed_ref[a * rank : (a + 1) * rank, :] = jnp.concatenate([part[:, lanes] for part in parts], axis=1)


def finish_kernel(summed, basis_ref, new_basis_ref, fresh_ref, wide, sketch):
    rank, width = basis_ref.shape[0], basis_ref.shape[1]
    lanes = basis_ref.shape[2]
    for a in range(rank):
        wide[a * width : (a + 1) * width, :] = basis_ref[a].astype(F32)
    group = 8

    def points(block, square):
        first = block * group
        acc = [jnp.zeros((rank, lanes), F32) for _ in range(group)]
        for a in range(rank):
            mixed = summed[a * rank : (a + 1) * rank, :]
            for j in range(group):
                acc[j] = acc[j] + wide[pl.ds(a * width + first + j, 1), :] * mixed
        for j in range(group):
            sketch[first + j] = acc[j]
            square = square + acc[j] * acc[j]
        return square

    square = lax.fori_loop(0, width // group, points, jnp.zeros((rank, lanes), F32))
    scale = lax.rsqrt(square / width + 1e-06)
    for p in range(width):
        new_basis_ref[p] = sketch[p] * scale

    def grams(block, carry):
        first = block * group

        acc = [jnp.zeros((rank, lanes), F32) for _ in range(group)]
        for p in range(width):
            row = sketch[p]
            for j in range(group):
                acc[j] = acc[j] + new_basis_ref[p, pl.ds(first + j, 1), :] * row
        for j in range(group):
            fresh_ref[first + j] = acc[j] / width
        return carry

    lax.fori_loop(0, rank // group, grams, 0)


def shards(
    samples,
    leaf_basis_matrix,
    transfer,
    leaf_lists,
    leaf_coupling,
    parent_lists,
    parent_coupling,
    test_matrix,
):
    rank, width, leaves = leaf_basis_matrix.shape
    vectors = samples.shape[0]
    parents = leaves // 2
    leaf_blocks, parent_blocks = leaf_lists.shape[0], parent_lists.shape[0]
    group = 16 if parents % 16 == 0 else parents
    chunks = parents // group
    leaf_sums, parent_sums = leaf_blocks * rank, parent_blocks * rank

    test = test_matrix.T
    product, summed = pl.pallas_call(
        functools.partial(sources_kernel, group),
        in_specs=[pl.BlockSpec(memory_space=pltpu.SMEM)] * 2 + [pl.BlockSpec(memory_space=pltpu.VMEM)] * 6,
        out_specs=[pl.BlockSpec(memory_space=pltpu.VMEM)] * 2,
        out_shape=[
            jax.ShapeDtypeStruct(samples.shape, BF16),
            jax.ShapeDtypeStruct((rank * rank, leaves), F32),
        ],
        scratch_shapes=[
            pltpu.VMEM((3, parents, rank + rank // 2, 2 * vectors), BF16),
            pltpu.VMEM((leaves * rank, width + rank), F32),
            pltpu.VMEM((3 * leaves, rank, 2 * vectors), BF16),
            pltpu.VMEM((3 * parents, rank, 2 * vectors), BF16),
            pltpu.VMEM((leaves * rank, 2 * vectors), F32),
            pltpu.VMEM((leaves * rank, leaf_sums), F32),
            pltpu.VMEM((parents * rank, parent_sums), F32),
            pltpu.VMEM((chunks, rank // chunks * rank, leaves), BF16),
            pltpu.VMEM((chunks, rank // chunks * rank, leaves), BF16),
            pltpu.SemaphoreType.DMA((2, chunks)),
            pltpu.SemaphoreType.DMA((2, chunks)),
            pltpu.SemaphoreType.DMA((chunks,)),
            pltpu.SemaphoreType.DMA((chunks,)),
        ],
        compiler_params=pltpu.CompilerParams(collective_id=0, has_side_effects=True),
        name="far_field",
    )(leaf_lists, parent_lists, samples, leaf_basis_matrix, transfer, leaf_coupling, parent_coupling, test)

    if lax.axis_size("vector") != 2:
        summed = lax.psum(summed, "vector")
    new_basis, fresh = pl.pallas_call(
        finish_kernel,
        in_specs=[pl.BlockSpec(memory_space=pltpu.VMEM)] * 2,
        out_specs=[pl.BlockSpec(memory_space=pltpu.VMEM)] * 2,
        out_shape=[
            jax.ShapeDtypeStruct((width, rank, leaves), F32),
            jax.ShapeDtypeStruct((rank, rank, leaves), F32),
        ],
        scratch_shapes=[
            pltpu.VMEM((rank * width, leaves), F32),
            pltpu.VMEM((width, rank, leaves), F32),
        ],
        name="finish",
    )(summed, leaf_basis_matrix)
    return product, new_basis, fresh


def solution(mesh):
    placed = (
        P("vector", LINE),
        P(None, None, LINE),
        P(None, None, LINE),
        P(None, LINE),
        P(None, None, None, LINE),
        P(None, LINE),
        P(None, None, None, LINE),
        P("vector", None),
    )
    return jax.shard_map(
        shards,
        mesh=mesh,
        in_specs=placed,
        out_specs=(P("vector", LINE), P(None, None, LINE), P(None, None, LINE)),
        check_vma=False,
    )
```

```python
import functools

import jax
import jax.numpy as jnp
from jax import lax
from jax.experimental import pallas as pl
from jax.experimental.pallas import tpu as pltpu
from jax.sharding import PartitionSpec as P

F32 = jnp.float32
BF16 = jnp.bfloat16
LINE = ("cluster", "replica")
TN = (((0,), (0,)), ((), ()))
NT = (((1,), (1,)), ((), ()))


def dot(a, b, dims=(((1,), (0,)), ((), ()))):
    return lax.dot_general(a, b, dims, preferred_element_type=F32)


def block_diagonal(pair):
    first, second = pair[0], pair[1]
    zero = jnp.zeros_like(first)
    return jnp.concatenate(
        [jnp.concatenate([first, zero], axis=1), jnp.concatenate([zero, second], axis=1)], axis=0
    )


def swap_halves(block):
    half = block.shape[1] // 2
    return jnp.concatenate([block[:, half:], block[:, :half]], axis=1)


def blocks_first(block):
    sources, blocks, targets = block.shape
    return jnp.swapaxes(block.astype(F32), 0, 1).reshape(blocks * sources, targets).T


def near(source, first, count):
    return jnp.minimum(jnp.maximum(source - first, 0), count - 1)


def sources_kernel(
    group,
    leaf_lists_ref,
    parent_lists_ref,
    samples_ref,
    basis_ref,
    transfer_ref,
    leaf_coupling_ref,
    parent_coupling_ref,
    test_ref,
    product_ref,
    summed_ref,
    coeff,
    mats,
    leaf_ext,
    parent_ext,
    totals,
    leaf_mats,
    parent_mats,
    own_packed,
    peer_packed,
    send_sem,
    recv_sem,
    packed_send_sem,
    packed_recv_sem,
):
    rank, each, leaves = basis_ref.shape
    parents = leaves // 2
    vectors = product_ref.shape[0]
    width = 2 * each
    paired = lax.axis_size("vector") == 2
    half = rank // 2
    chunks = parents // group
    leaf_blocks, parent_blocks = leaf_lists_ref.shape[0], parent_lists_ref.shape[0]

    replicas = lax.axis_size("replica")
    size = lax.axis_size("cluster") * replicas
    here = lax.axis_index("cluster") * replicas + lax.axis_index("replica")
    vector = lax.axis_index("vector")

    def device(place):
        return (place // replicas, vector, lax.rem(place, replicas))

    right = device(lax.rem(here + 1, size))
    left = device(lax.rem(here + size - 1, size))

    barrier = pltpu.get_barrier_semaphore()
    peer = (lax.axis_index("cluster"), 1 - vector, lax.axis_index("replica"))
    greeted = (left, right, peer) if paired else (left, right)
    for neighbour in greeted:
        pl.semaphore_signal(barrier, inc=1, device_id=neighbour, device_id_type=pl.DeviceIdType.MESH)

    def by_leaf(block, carry):
        for u in range(4):
            r = block * 4 + u
            both = jnp.concatenate([basis_ref[r], transfer_ref[r]], axis=0).astype(F32)
            mats[pl.ds(r, leaves, stride=rank), :] = both.T
        return carry

    lax.fori_loop(0, rank // 4, by_leaf, 0)
    pl.semaphore_wait(barrier, len(greeted))

    def pair_of(q):
        return mats[pl.ds(pl.multiple_of(q * 2 * rank, 2 * rank), 2 * rank), :].astype(BF16)

    def bases(q):
        pair = pair_of(q)[:, :each]
        return block_diagonal((pair[:rank], pair[rank:]))

    def lift(q):
        return pair_of(q)[:, each:]

    def line_copy(way, chunk):
        rows = pl.ds(chunk * group, group)
        return pltpu.make_async_remote_copy(
            src_ref=coeff.at[1, rows],
            dst_ref=coeff.at[2 * way, rows],
            send_sem=send_sem.at[way, chunk],
            recv_sem=recv_sem.at[way, chunk],
            device_id=(right, left)[way],
            device_id_type=pl.DeviceIdType.MESH,
        )

    def packed_copy(chunk):
        return pltpu.make_async_remote_copy(
            src_ref=own_packed.at[chunk],
            dst_ref=peer_packed.at[chunk],
            send_sem=packed_send_sem.at[chunk],
            recv_sem=packed_recv_sem.at[chunk],
            device_id=peer,
            device_id_type=pl.DeviceIdType.MESH,
        )

    def coefficients(chunk):
        leaf, parent = [], []
        for j in range(group):
            q = chunk * group + j
            points = samples_ref[:, pl.ds(pl.multiple_of(q * width, width), width)]
            leaf.append(dot(bases(q), points, NT).astype(BF16))
        for j in range(group):
            parent.append(dot(lift(chunk * group + j), leaf[j], TN).astype(BF16))
        for j in range(group):
            q = chunk * group + j
            coeff[1, q, :rank, :] = jnp.concatenate([leaf[j][:rank], leaf[j][rank:]], axis=1)
            coeff[1, q, rank:, :] = jnp.concatenate([parent[j][:half], parent[j][half:]], axis=1)

    orders = (list(range(chunks))[::-1], list(range(chunks)))
    ready, sent = set(), [0, 0]
    for turn in range(chunks):
        chunk = turn // 2 if turn % 2 else chunks - 1 - turn // 2
        coefficients(chunk)
        ready.add(chunk)
        progress = True
        while progress:
            progress = False
            for way in range(2):
                if sent[way] < chunks and orders[way][sent[way]] in ready:
                    line_copy(way, orders[way][sent[way]]).start()
                    sent[way] += 1
                    progress = True

    def relayout(block, carry):
        for u in range(4):
            r = block * 4 + u
            leaf_mats[pl.ds(r, leaves, stride=rank), :] = blocks_first(leaf_coupling_ref[r])
            parent_mats[pl.ds(r, parents, stride=rank), :] = blocks_first(parent_coupling_ref[r])
        return carry

    lax.fori_loop(0, rank // 4, relayout, 0)

    def unpack(place, first, many):
        def some(block, carry):
            for u in range(8):
                q = first + block * 8 + u
                target = place * parents + q
                pair = coeff[place, q, :rank, :]
                up = coeff[place, q, rank:, :]
                leaf_ext[2 * target] = pair
                leaf_ext[2 * target + 1] = swap_halves(pair)
                parent_ext[target, :half, :] = up
                parent_ext[target, half:, :] = swap_halves(up)
            return carry

        lax.fori_loop(0, many // 8, some, 0)

    unpack(1, 0, parents)

    leaf_first, parent_first = (here - 1) * leaves, (here - 1) * parents

    def far_field(chunk, carry):
        leaf_far, parent_far, total = [], [], []
        for j in range(group):
            q = chunk * group + j
            for c in range(2):
                t = 2 * q + c
                source = jnp.concatenate(
                    [leaf_ext[near(leaf_lists_ref[k, t], leaf_first, 3 * leaves)] for k in range(leaf_blocks)], axis=0
                )
                mats = leaf_mats[pl.ds(pl.multiple_of(t * rank, rank), rank), :].astype(BF16)
                leaf_far.append(dot(mats, source))
            source = jnp.concatenate(
                [parent_ext[near(parent_lists_ref[k, q], parent_first, 3 * parents)] for k in range(parent_blocks)],
                axis=0,
            )
            mats = parent_mats[pl.ds(pl.multiple_of(q * rank, rank), rank), :].astype(BF16)
            parent_far.append(dot(mats, source).astype(BF16))
        descend = [dot(lift(chunk * group + j), parent_far[j]) for j in range(group)]
        for j in range(group):
            far = jnp.concatenate(leaf_far[2 * j : 2 * j + 2], axis=0)
            total.append((far + descend[j]).astype(BF16))
        for j in range(group):
            q = chunk * group + j
            columns = pl.ds(pl.multiple_of(q * width, width), width)
            product_ref[:, columns] = dot(total[j][:, :vectors], bases(q), TN).astype(BF16)
        for j in range(group):
            q = chunk * group + j
            totals[pl.ds(pl.multiple_of(q * 2 * rank, 2 * rank), 2 * rank), :] = total[j].astype(F32)
        first = chunk * (group * 2 * rank)
        for block in range(rank // chunks):
            mine = jnp.concatenate(
                [totals[pl.ds(first + block * chunks + j, 2 * group, stride=rank), :] for j in range(chunks)], axis=0
            )
            mine = mine[:, :vectors].astype(BF16)
            own_packed[chunk, block * rank : (block + 1) * rank, :] = dot(test_ref[...], mine, NT).astype(BF16)
        if paired:
            packed_copy(chunk).start()
        return carry

    arrived = 0
    for reach in range(chunks // 2 + 1, chunks + 1):
        for turn in range(arrived, reach):
            for way in range(2):
                chunk = orders[way][turn]
                line_copy(way, chunk).wait()
                unpack(2 * way, chunk * group, group)
        arrived = reach
        low, high = chunks - reach, reach - 1
        lax.fori_loop(0, 1 if low == high else 2, lambda i, c: far_field(low + i * (high - low), c), 0)

    if paired:
        for chunk in range(chunks):
            packed_copy(chunk).wait()
    for block in range(rank // chunks):
        rows = slice(block * rank, (block + 1) * rank)
        parts = [own_packed[chunk, rows, :].astype(F32) for chunk in range(chunks)]
        if paired:
            parts = [parts[chunk] + peer_packed[chunk, rows, :].astype(F32) for chunk in range(chunks)]
        for j in range(chunks):
            lanes = slice(j * 2 * group, (j + 1) * 2 * group)
            a = block * chunks + j
            summed_ref[a * rank : (a + 1) * rank, :] = jnp.concatenate([part[:, lanes] for part in parts], axis=1)


def finish_kernel(summed, basis_ref, new_basis_ref, fresh_ref, wide, sketch):
    rank, width = basis_ref.shape[0], basis_ref.shape[1]
    lanes = basis_ref.shape[2]
    for a in range(rank):
        wide[a * width : (a + 1) * width, :] = basis_ref[a].astype(F32)
    group = 8

    def points(block, square):
        first = block * group
        acc = [jnp.zeros((rank, lanes), F32) for _ in range(group)]
        for a in range(rank):
            mixed = summed[a * rank : (a + 1) * rank, :]
            for j in range(group):
                acc[j] = acc[j] + wide[pl.ds(a * width + first + j, 1), :] * mixed
        for j in range(group):
            sketch[first + j] = acc[j]
            square = square + acc[j] * acc[j]
        return square

    square = lax.fori_loop(0, width // group, points, jnp.zeros((rank, lanes), F32))
    scale = lax.rsqrt(square / width + 1e-06)
    for p in range(width):
        new_basis_ref[p] = sketch[p] * scale

    def grams(block, carry):
        first = block * group

        acc = [jnp.zeros((rank, lanes), F32) for _ in range(group)]
        for p in range(width):
            row = sketch[p]
            for j in range(group):
                acc[j] = acc[j] + new_basis_ref[p, pl.ds(first + j, 1), :] * row
        for j in range(group):
            fresh_ref[first + j] = acc[j] / width
        return carry

    lax.fori_loop(0, rank // group, grams, 0)


def shards(
    samples,
    leaf_basis_matrix,
    transfer,
    leaf_lists,
    leaf_coupling,
    parent_lists,
    parent_coupling,
    test_matrix,
):
    rank, width, leaves = leaf_basis_matrix.shape
    vectors = samples.shape[0]
    parents = leaves // 2
    leaf_blocks, parent_blocks = leaf_lists.shape[0], parent_lists.shape[0]
    group = 16 if parents % 16 == 0 else parents
    chunks = parents // group
    leaf_sums, parent_sums = leaf_blocks * rank, parent_blocks * rank

    test = test_matrix.T
    product, summed = pl.pallas_call(
        functools.partial(sources_kernel, group),
        in_specs=[pl.BlockSpec(memory_space=pltpu.SMEM)] * 2 + [pl.BlockSpec(memory_space=pltpu.VMEM)] * 6,
        out_specs=[pl.BlockSpec(memory_space=pltpu.VMEM)] * 2,
        out_shape=[
            jax.ShapeDtypeStruct(samples.shape, BF16),
            jax.ShapeDtypeStruct((rank * rank, leaves), F32),
        ],
        scratch_shapes=[
            pltpu.VMEM((3, parents, rank + rank // 2, 2 * vectors), BF16),
            pltpu.VMEM((leaves * rank, width + rank), F32),
            pltpu.VMEM((3 * leaves, rank, 2 * vectors), BF16),
            pltpu.VMEM((3 * parents, rank, 2 * vectors), BF16),
            pltpu.VMEM((leaves * rank, 2 * vectors), F32),
            pltpu.VMEM((leaves * rank, leaf_sums), F32),
            pltpu.VMEM((parents * rank, parent_sums), F32),
            pltpu.VMEM((chunks, rank // chunks * rank, leaves), BF16),
            pltpu.VMEM((chunks, rank // chunks * rank, leaves), BF16),
            pltpu.SemaphoreType.DMA((2, chunks)),
            pltpu.SemaphoreType.DMA((2, chunks)),
            pltpu.SemaphoreType.DMA((chunks,)),
            pltpu.SemaphoreType.DMA((chunks,)),
        ],
        compiler_params=pltpu.CompilerParams(collective_id=0, has_side_effects=True),
        name="far_field",
    )(leaf_lists, parent_lists, samples, leaf_basis_matrix, transfer, leaf_coupling, parent_coupling, test)

    if lax.axis_size("vector") != 2:
        summed = lax.psum(summed, "vector")
    new_basis, fresh = pl.pallas_call(
        finish_kernel,
        in_specs=[pl.BlockSpec(memory_space=pltpu.VMEM)] * 2,
        out_specs=[pl.BlockSpec(memory_space=pltpu.VMEM)] * 2,
        out_shape=[
            jax.ShapeDtypeStruct((width, rank, leaves), F32),
            jax.ShapeDtypeStruct((rank, rank, leaves), F32),
        ],
        scratch_shapes=[
            pltpu.VMEM((rank * width, leaves), F32),
            pltpu.VMEM((width, rank, leaves), F32),
        ],
        name="finish",
    )(summed, leaf_basis_matrix)
    return product, new_basis, fresh


def solution(mesh):
    placed = (
        P("vector", LINE),
        P(None, None, LINE),
        P(None, None, LINE),
        P(None, LINE),
        P(None, None, None, LINE),
        P(None, LINE),
        P(None, None, None, LINE),
        P("vector", None),
    )
    return jax.shard_map(
        shards,
        mesh=mesh,
        in_specs=placed,
        out_specs=(P("vector", LINE), P(None, None, LINE), P(None, None, LINE)),
        check_vma=False,
    )
```

```python
import functools

import jax
import jax.numpy as jnp
from jax import lax
from jax.experimental import pallas as pl
from jax.experimental.pallas import tpu as pltpu
from jax.sharding import PartitionSpec as P

F32 = jnp.float32
BF16 = jnp.bfloat16
LINE = ("cluster", "replica")
TN = (((0,), (0,)), ((), ()))
NT = (((1,), (1,)), ((), ()))


def dot(a, b, dims=(((1,), (0,)), ((), ()))):
    return lax.dot_general(a, b, dims, preferred_element_type=F32)


def block_diagonal(pair):
    first, second = pair[0], pair[1]
    zero = jnp.zeros_like(first)
    return jnp.concatenate(
        [jnp.concatenate([first, zero], axis=1), jnp.concatenate([zero, second], axis=1)], axis=0
    )


def swap_halves(block):
    half = block.shape[1] // 2
    return jnp.concatenate([block[:, half:], block[:, :half]], axis=1)


def blocks_first(block):
    sources, blocks, targets = block.shape
    return jnp.swapaxes(block.astype(F32), 0, 1).reshape(blocks * sources, targets).T


def near(source, first, count):
    return jnp.minimum(jnp.maximum(source - first, 0), count - 1)


def sources_kernel(
    group,
    leaf_lists_ref,
    parent_lists_ref,
    samples_ref,
    basis_ref,
    transfer_ref,
    leaf_coupling_ref,
    parent_coupling_ref,
    test_ref,
    product_ref,
    summed_ref,
    coeff,
    mats,
    leaf_ext,
    parent_ext,
    totals,
    leaf_mats,
    parent_mats,
    own_packed,
    peer_packed,
    send_sem,
    recv_sem,
    packed_send_sem,
    packed_recv_sem,
):
    rank, each, leaves = basis_ref.shape
    parents = leaves // 2
    vectors = product_ref.shape[0]
    width = 2 * each
    paired = lax.axis_size("vector") == 2
    half = rank // 2
    chunks = parents // group
    leaf_blocks, parent_blocks = leaf_lists_ref.shape[0], parent_lists_ref.shape[0]

    replicas = lax.axis_size("replica")
    size = lax.axis_size("cluster") * replicas
    here = lax.axis_index("cluster") * replicas + lax.axis_index("replica")
    vector = lax.axis_index("vector")

    def device(place):
        return (place // replicas, vector, lax.rem(place, replicas))

    right = device(lax.rem(here + 1, size))
    left = device(lax.rem(here + size - 1, size))

    barrier = pltpu.get_barrier_semaphore()
    peer = (lax.axis_index("cluster"), 1 - vector, lax.axis_index("replica"))
    greeted = (left, right, peer) if paired else (left, right)
    for neighbour in greeted:
        pl.semaphore_signal(barrier, inc=1, device_id=neighbour, device_id_type=pl.DeviceIdType.MESH)

    def by_leaf(block, carry):
        for u in range(4):
            r = block * 4 + u
            both = jnp.concatenate([basis_ref[r], transfer_ref[r]], axis=0).astype(F32)
            mats[pl.ds(r, leaves, stride=rank), :] = both.T
        return carry

    lax.fori_loop(0, rank // 4, by_leaf, 0)
    pl.semaphore_wait(barrier, len(greeted))

    def pair_of(q):
        return mats[pl.ds(pl.multiple_of(q * 2 * rank, 2 * rank), 2 * rank), :].astype(BF16)

    def bases(q):
        pair = pair_of(q)[:, :each]
        return block_diagonal((pair[:rank], pair[rank:]))

    def lift(q):
        return pair_of(q)[:, each:]

    def line_copy(way, chunk):
        rows = pl.ds(chunk * group, group)
        return pltpu.make_async_remote_copy(
            src_ref=coeff.at[1, rows],
            dst_ref=coeff.at[2 * way, rows],
            send_sem=send_sem.at[way, chunk],
            recv_sem=recv_sem.at[way, chunk],
            device_id=(right, left)[way],
            device_id_type=pl.DeviceIdType.MESH,
        )

    def packed_copy(chunk):
        return pltpu.make_async_remote_copy(
            src_ref=own_packed.at[chunk],
            dst_ref=peer_packed.at[chunk],
            send_sem=packed_send_sem.at[chunk],
            recv_sem=packed_recv_sem.at[chunk],
            device_id=peer,
            device_id_type=pl.DeviceIdType.MESH,
        )

    def coefficients(chunk):
        leaf, parent = [], []
        for j in range(group):
            q = chunk * group + j
            points = samples_ref[:, pl.ds(pl.multiple_of(q * width, width), width)]
            leaf.append(dot(bases(q), points, NT).astype(BF16))
        for j in range(group):
            parent.append(dot(lift(chunk * group + j), leaf[j], TN).astype(BF16))
        for j in range(group):
            q = chunk * group + j
            coeff[1, q, :rank, :] = jnp.concatenate([leaf[j][:rank], leaf[j][rank:]], axis=1)
            coeff[1, q, rank:, :] = jnp.concatenate([parent[j][:half], parent[j][half:]], axis=1)

    orders = (list(range(chunks))[::-1], list(range(chunks)))
    ready, sent = set(), [0, 0]
    for turn in range(chunks):
        chunk = turn // 2 if turn % 2 else chunks - 1 - turn // 2
        coefficients(chunk)
        ready.add(chunk)
        progress = True
        while progress:
            progress = False
            for way in range(2):
                if sent[way] < chunks and orders[way][sent[way]] in ready:
                    line_copy(way, orders[way][sent[way]]).start()
                    sent[way] += 1
                    progress = True

    def relayout(block, carry):
        for u in range(4):
            r = block * 4 + u
            leaf_mats[pl.ds(r, leaves, stride=rank), :] = blocks_first(leaf_coupling_ref[r])
            parent_mats[pl.ds(r, parents, stride=rank), :] = blocks_first(parent_coupling_ref[r])
        return carry

    lax.fori_loop(0, rank // 4, relayout, 0)

    def unpack(place, first, many):
        def some(block, carry):
            for u in range(8):
                q = first + block * 8 + u
                target = place * parents + q
                pair = coeff[place, q, :rank, :]
                up = coeff[place, q, rank:, :]
                leaf_ext[2 * target] = pair
                leaf_ext[2 * target + 1] = swap_halves(pair)
                parent_ext[target, :half, :] = up
                parent_ext[target, half:, :] = swap_halves(up)
            return carry

        lax.fori_loop(0, many // 8, some, 0)

    unpack(1, 0, parents)

    leaf_first, parent_first = (here - 1) * leaves, (here - 1) * parents

    def far_field(chunk, carry):
        leaf_far, parent_far, total = [], [], []
        for j in range(group):
            q = chunk * group + j
            for c in range(2):
                t = 2 * q + c
                source = jnp.concatenate(
                    [leaf_ext[near(leaf_lists_ref[k, t], leaf_first, 3 * leaves)] for k in range(leaf_blocks)], axis=0
                )
                mats = leaf_mats[pl.ds(pl.multiple_of(t * rank, rank), rank), :].astype(BF16)
                leaf_far.append(dot(mats, source))
            source = jnp.concatenate(
                [parent_ext[near(parent_lists_ref[k, q], parent_first, 3 * parents)] for k in range(parent_blocks)],
                axis=0,
            )
            mats = parent_mats[pl.ds(pl.multiple_of(q * rank, rank), rank), :].astype(BF16)
            parent_far.append(dot(mats, source).astype(BF16))
        descend = [dot(lift(chunk * group + j), parent_far[j]) for j in range(group)]
        for j in range(group):
            far = jnp.concatenate(leaf_far[2 * j : 2 * j + 2], axis=0)
            total.append((far + descend[j]).astype(BF16))
        for j in range(group):
            q = chunk * group + j
            columns = pl.ds(pl.multiple_of(q * width, width), width)
            product_ref[:, columns] = dot(total[j][:, :vectors], bases(q), TN).astype(BF16)
        for j in range(group):
            q = chunk * group + j
            totals[pl.ds(pl.multiple_of(q * 2 * rank, 2 * rank), 2 * rank), :] = total[j].astype(F32)
        first = chunk * (group * 2 * rank)
        for block in range(rank // chunks):
            mine = jnp.concatenate(
                [totals[pl.ds(first + block * chunks + j, 2 * group, stride=rank), :] for j in range(chunks)], axis=0
            )
            mine = mine[:, :vectors].astype(BF16)
            own_packed[chunk, block * rank : (block + 1) * rank, :] = dot(test_ref[...], mine, NT).astype(BF16)
        if paired:
            packed_copy(chunk).start()
        return carry

    arrived = 0
    for reach in range(chunks // 2 + 1, chunks + 1):
        for turn in range(arrived, reach):
            for way in range(2):
                chunk = orders[way][turn]
                line_copy(way, chunk).wait()
                unpack(2 * way, chunk * group, group)
        arrived = reach
        low, high = chunks - reach, reach - 1
        lax.fori_loop(0, 1 if low == high else 2, lambda i, c: far_field(low + i * (high - low), c), 0)

    if paired:
        for chunk in range(chunks):
            packed_copy(chunk).wait()
    for block in range(rank // chunks):
        rows = slice(block * rank, (block + 1) * rank)
        parts = [own_packed[chunk, rows, :].astype(F32) for chunk in range(chunks)]
        if paired:
            parts = [parts[chunk] + peer_packed[chunk, rows, :].astype(F32) for chunk in range(chunks)]
        for j in range(chunks):
            lanes = slice(j * 2 * group, (j + 1) * 2 * group)
            a = block * chunks + j
            summed_ref[a * rank : (a + 1) * rank, :] = jnp.concatenate([part[:, lanes] for part in parts], axis=1)


def finish_kernel(summed, basis_ref, new_basis_ref, fresh_ref, wide, sketch, scales, inverses):
    rank, width = basis_ref.shape[0], basis_ref.shape[1]
    lanes = basis_ref.shape[2]
    for a in range(rank):
        wide[a * width : (a + 1) * width, :] = basis_ref[a].astype(F32)
    group = 8

    def points(block, square):
        first = block * group
        acc = [jnp.zeros((rank, lanes), F32) for _ in range(group)]
        for a in range(rank):
            mixed = summed[a * rank : (a + 1) * rank, :]
            for j in range(group):
                acc[j] = acc[j] + wide[pl.ds(a * width + first + j, 1), :] * mixed
        for j in range(group):
            sketch[first + j] = acc[j]
            square = square + acc[j] * acc[j]
        return square

    square = lax.fori_loop(0, width // group, points, jnp.zeros((rank, lanes), F32))
    scale = lax.rsqrt(square / width + 1e-06)
    for p in range(width):
        new_basis_ref[p] = sketch[p] * scale

    scales[...] = scale
    inverses[...] = jnp.sqrt(square / width + 1e-06)
    for block in range(rank // group):
        first = block * group

        def grams(part, acc):
            acc = list(acc)
            for u in range(group):
                p = part * group + u
                row = sketch[p, first:, :]
                for j in range(group):
                    acc[j] = acc[j] + new_basis_ref[p, first + j : first + j + 1, :] * row
            return tuple(acc)

        start = tuple(jnp.zeros((rank - first, lanes), F32) for _ in range(group))
        acc = lax.fori_loop(0, width // group, grams, start)
        later = first + group
        for j in range(group):
            a = first + j
            here = acc[j] / width
            fresh_ref[a, first:, :] = here
            if later < rank:
                turned = here[group:] * scales[later:, :] * inverses[a : a + 1, :]
                flat = fresh_ref.reshape(rank * rank, lanes)
                flat[pl.ds(later * rank + a, rank - later, stride=rank), :] = turned


def shards(
    samples,
    leaf_basis_matrix,
    transfer,
    leaf_lists,
    leaf_coupling,
    parent_lists,
    parent_coupling,
    test_matrix,
):
    rank, width, leaves = leaf_basis_matrix.shape
    vectors = samples.shape[0]
    parents = leaves // 2
    leaf_blocks, parent_blocks = leaf_lists.shape[0], parent_lists.shape[0]
    group = 16 if parents % 16 == 0 else parents
    chunks = parents // group
    leaf_sums, parent_sums = leaf_blocks * rank, parent_blocks * rank

    test = test_matrix.T
    product, summed = pl.pallas_call(
        functools.partial(sources_kernel, group),
        in_specs=[pl.BlockSpec(memory_space=pltpu.SMEM)] * 2 + [pl.BlockSpec(memory_space=pltpu.VMEM)] * 6,
        out_specs=[pl.BlockSpec(memory_space=pltpu.VMEM)] * 2,
        out_shape=[
            jax.ShapeDtypeStruct(samples.shape, BF16),
            jax.ShapeDtypeStruct((rank * rank, leaves), F32),
        ],
        scratch_shapes=[
            pltpu.VMEM((3, parents, rank + rank // 2, 2 * vectors), BF16),
            pltpu.VMEM((leaves * rank, width + rank), F32),
            pltpu.VMEM((3 * leaves, rank, 2 * vectors), BF16),
            pltpu.VMEM((3 * parents, rank, 2 * vectors), BF16),
            pltpu.VMEM((leaves * rank, 2 * vectors), F32),
            pltpu.VMEM((leaves * rank, leaf_sums), F32),
            pltpu.VMEM((parents * rank, parent_sums), F32),
            pltpu.VMEM((chunks, rank // chunks * rank, leaves), BF16),
            pltpu.VMEM((chunks, rank // chunks * rank, leaves), BF16),
            pltpu.SemaphoreType.DMA((2, chunks)),
            pltpu.SemaphoreType.DMA((2, chunks)),
            pltpu.SemaphoreType.DMA((chunks,)),
            pltpu.SemaphoreType.DMA((chunks,)),
        ],
        compiler_params=pltpu.CompilerParams(collective_id=0, has_side_effects=True),
        name="far_field",
    )(leaf_lists, parent_lists, samples, leaf_basis_matrix, transfer, leaf_coupling, parent_coupling, test)

    if lax.axis_size("vector") != 2:
        summed = lax.psum(summed, "vector")
    new_basis, fresh = pl.pallas_call(
        finish_kernel,
        in_specs=[pl.BlockSpec(memory_space=pltpu.VMEM)] * 2,
        out_specs=[pl.BlockSpec(memory_space=pltpu.VMEM)] * 2,
        out_shape=[
            jax.ShapeDtypeStruct((width, rank, leaves), F32),
            jax.ShapeDtypeStruct((rank, rank, leaves), F32),
        ],
        scratch_shapes=[
            pltpu.VMEM((rank * width, leaves), F32),
            pltpu.VMEM((width, rank, leaves), F32),
            pltpu.VMEM((rank, leaves), F32),
            pltpu.VMEM((rank, leaves), F32),
        ],
        name="finish",
    )(summed, leaf_basis_matrix)
    return product, new_basis, fresh


def solution(mesh):
    placed = (
        P("vector", LINE),
        P(None, None, LINE),
        P(None, None, LINE),
        P(None, LINE),
        P(None, None, None, LINE),
        P(None, LINE),
        P(None, None, None, LINE),
        P("vector", None),
    )
    return jax.shard_map(
        shards,
        mesh=mesh,
        in_specs=placed,
        out_specs=(P("vector", LINE), P(None, None, LINE), P(None, None, LINE)),
        check_vma=False,
    )
```
